128 devices in a mesh: tok: 16 (over z, x_lo, core), col: 8 (over y, x_hi).
Axes of the slice: x: 4 (x_hi: 2, x_lo: 2; x = x_hi * 2 + x_lo), y: 4, z: 4, core: 2. Of those that a mesh axis runs over, the one named last changes fastest.
Arguments:
- tokens: bfloat16 [16384, 4096], P('tok'), may hold values from -6 to 6
- grads_out: bfloat16 [16384, 8192], P('tok', 'col'), may hold values from -0.046875 to 0.046875
- statistics: float32 [8, 16, 1024, 512], P('col', 'tok'), as said below
Outputs:
- update: bfloat16 [4096, 8192], P('tok', 'col')
- new_statistics: float32 [8, 16, 1024, 512], P('col', 'tok')
The draws below stay inside these ranges and needn't reach their ends.
Inputs may be any that keep to these rules, and one draw needn't show every extreme that they name: statistics[j, (2 i + s) * 2 + w] holds columns w * 512 onward of a symmetric positive definite matrix with a positive diagonal.
All inputs are finite; a program needn't handle non-finite values.
Results may differ from the reference program's by a relative error of at most 0.007.
Values may be sent and summed in bfloat16 or wider, within the bound.
No kernel may reach another device: no remote copies, remote signals or barrier semaphores. Data moves between devices by JAX's collectives and lax.ppermute only.
A program may use at most 128 MiB of HBM per device.

```python
import math
import jax
import jax.numpy as jnp
from jax import lax

D = 4096
QUERY = 8192
ORDER = 1024
ITERS = 3
TOKENS = 16384
ROW_BLOCKS = 4
COL_BLOCKS = 8
PIECES = 2
N_TOK = 16


def draw_statistics(key, part):
    number_mats = COL_BLOCKS * ROW_BLOCKS * 2

    def one_matrix(seed_key):
        key_base, key_diag = jax.random.split(seed_key)
        base = jax.random.normal(key_base, (ORDER, ORDER), jnp.float32)
        rank_index = jnp.arange(1, ORDER + 1, dtype=jnp.float32)
        exponent = 1.0
        diagonal = jnp.exp(jax.random.uniform(key_diag, (ORDER,), jnp.float32, math.log(0.25 * ORDER), math.log(2.0 * ORDER)))
        strengths = 64.0 * ORDER * jnp.power(rank_index, -exponent)
        weighted = base * strengths[None, :]
        return jnp.dot(weighted, base.T, precision=lax.Precision.HIGHEST) / ORDER + jnp.diag(diagonal)
    matrices = lax.map(one_matrix, jax.random.split(jax.random.fold_in(key, 17), number_mats))
    matrices = matrices.reshape(COL_BLOCKS, ROW_BLOCKS, 2, ORDER, PIECES, ORDER // PIECES)
    return jnp.transpose(matrices, (0, 1, 2, 4, 3, 5)).reshape(COL_BLOCKS, 2 * ROW_BLOCKS * PIECES, ORDER, ORDER // PIECES)


def levels(rng, extent, cuts, smallest, high):
    def one(axis_at, shards_of):
        draws = jax.random.uniform(jax.random.fold_in(jax.random.fold_in(rng, 6), axis_at), (shards_of,), jnp.float32, smallest / len(cuts), high / len(cuts))
        return jnp.repeat(jnp.exp(draws), extent[axis_at] // shards_of).reshape((-1,) + (1,) * (len(extent) - axis_at - 1))

    factor_of = one(*cuts[0])
    for cut in cuts[1:]:
        factor_of = factor_of * one(*cut)
    return factor_of


def centred(own_key, shape, width, limit, cuts=(), kind=jnp.bfloat16):
    level = levels(own_key, shape, cuts, -0.22, 0.18) if cuts else 1.0
    array = jax.random.normal(own_key, shape, jnp.float32) * width * level
    return jnp.minimum(jnp.maximum(array, -limit), limit).astype(kind)


def setup_inputs(seed: int = 0) -> dict:
    splits = jax.random.split(jax.random.key(seed), 4)
    return {
        "tokens": centred(splits[0], (TOKENS, D), 1.0, 6.0, ((0, 16),)),
        "grads_out": centred(splits[1], (TOKENS, QUERY), TOKENS ** -0.5, 0.046875, ((0, 16), (1, 8))),
        "statistics": draw_statistics(jax.random.fold_in(splits[3], 71), 0),
    }


def inverse_root(statistic):
    identity = jnp.eye(statistic.shape[0], dtype=jnp.float32)
    scaling = 2.5 / jnp.sqrt(jnp.sum(statistic * statistic) + 1e-06)
    matrix = scaling * statistic
    factor = (5.0 * identity - matrix) * 0.25
    iterate = jnp.sqrt(jnp.sqrt(scaling)) * factor
    for repeat in range(1, ITERS):
        square = jnp.dot(factor, factor, precision=lax.Precision.HIGHEST)
        fourth = jnp.dot(square, square, precision=lax.Precision.HIGHEST)
        matrix = jnp.dot(fourth, matrix, precision=lax.Precision.HIGHEST)
        factor = (5.0 * identity - matrix) * 0.25
        iterate = jnp.dot(factor, iterate, precision=lax.Precision.HIGHEST)
    return iterate

def reference(tokens, grads_out, statistics):
    pieces = N_TOK // (2 * ROW_BLOCKS)
    assembled = statistics.reshape(COL_BLOCKS, ROW_BLOCKS, 2, pieces, ORDER, ORDER // pieces)
    assembled = jnp.transpose(assembled, (0, 1, 2, 4, 3, 5)).reshape(COL_BLOCKS, ROW_BLOCKS, 2, ORDER, ORDER)
    scale_factor = math.sqrt(ORDER)

    def one_column(column_index):
        columns = lax.dynamic_slice_in_dim(grads_out, column_index * ORDER, ORDER, 1)
        gradient = lax.dot_general(tokens, columns, (((0,), (0,)), ((), ())), preferred_element_type=jnp.float32)
        grad_blocks = gradient.astype(jnp.bfloat16).reshape(ROW_BLOCKS, ORDER, ORDER)
        previous = lax.dynamic_index_in_dim(assembled, column_index, 0, keepdims=False)

        def one_block(inputs_pair):
            grad_block, old_stats = inputs_pair
            left_stat = old_stats[0] + jnp.dot(grad_block, grad_block.T, preferred_element_type=jnp.float32)
            right_stat = old_stats[1] + jnp.dot(grad_block.T, grad_block, preferred_element_type=jnp.float32)
            left_root = inverse_root(left_stat).astype(jnp.bfloat16)
            right_root = inverse_root(right_stat).astype(jnp.bfloat16)
            mixed_rows = jnp.dot(left_root, grad_block, preferred_element_type=jnp.float32).astype(jnp.bfloat16)
            update = (jnp.dot(mixed_rows, right_root, preferred_element_type=jnp.float32) * scale_factor).astype(jnp.bfloat16)
            return (update, jnp.stack([left_stat, right_stat]))
        return lax.map(one_block, (grad_blocks, previous))
    updates, fresh_stats = lax.map(one_column, jnp.arange(COL_BLOCKS, dtype=jnp.int32))
    update = jnp.transpose(updates, (1, 2, 0, 3)).reshape(ROW_BLOCKS * ORDER, COL_BLOCKS * ORDER)
    fresh_stats = fresh_stats.reshape(COL_BLOCKS, ROW_BLOCKS, 2, ORDER, pieces, ORDER // pieces)
    fresh_stats = jnp.transpose(fresh_stats, (0, 1, 2, 4, 3, 5)).reshape(COL_BLOCKS, ROW_BLOCKS * 2 * pieces, ORDER, ORDER // pieces)
    return (update, fresh_stats)
```

```python
import math

import jax
import jax.numpy as jnp
from jax import lax
from jax.sharding import PartitionSpec as P

ITERS = 3
CHUNKS = 2


def swapped(block, axis, bit):
    count = lax.axis_size(axis)
    route = []
    for low in range(count):
        high = low | 1 << bit
        if high != low and high < count:
            route += [(low, high), (high, low)]
    return lax.ppermute(block, axis, route)


def ring_sent(block, axis, stride):
    count = lax.axis_size(axis)
    route = []
    for source in range(count):
        step = stride if source % 2 == 0 else -stride
        route.append((source, (source + step) % count))
    return lax.ppermute(block, axis, route)


def summed_gradient(tokens, grads_out, device):
    count = lax.axis_size("tok")
    stride = 4
    ring = count // stride
    core = device % 2
    place = device // stride
    order = grads_out.shape[1]
    half = order // 2
    rows = order // CHUNKS
    own_grads = lax.dynamic_slice_in_dim(grads_out, core * half, half, 1)
    mate_grads = lax.dynamic_slice_in_dim(grads_out, (1 - core) * half, half, 1)
    turn = 1 - 2 * core

    def partial(block, chunk, grads, size):
        start = block * order + chunk * size
        picked = lax.dynamic_slice_in_dim(tokens, start, size, 1)
        return lax.dot_general(
            picked, grads, (((0,), (0,)), ((), ())), preferred_element_type=jnp.float32
        )

    travelling = [None] * CHUNKS
    for step in range(1, ring + 1):
        own_block = (place - turn * step) % ring
        mate_block = (place + turn * step) % ring
        for chunk in range(CHUNKS):
            given = partial(mate_block, chunk, mate_grads, rows).astype(jnp.bfloat16)
            received = swapped(given, "tok", 0)
            total = partial(own_block, chunk, own_grads, rows) + received.astype(jnp.float32)
            if travelling[chunk] is not None:
                total = total + travelling[chunk].astype(jnp.float32)
            total = total.astype(jnp.bfloat16)
            if step < ring:
                total = ring_sent(total, "tok", stride)
            travelling[chunk] = total
    result = []
    for chunk in range(CHUNKS):
        across = swapped(travelling[chunk], "tok", 1)
        result.append(
            (travelling[chunk].astype(jnp.float32) + across.astype(jnp.float32)).astype(
                jnp.bfloat16
            )
        )
    return result


def doubling(values, levels, device, axis_dim, partner):
    for level_bit in range(levels):
        partner_part = partner(values, level_bit)
        low_side = device // 2**level_bit % 2 == 0
        values = jnp.where(
            low_side,
            jnp.concatenate([values, partner_part], axis_dim),
            jnp.concatenate([partner_part, values], axis_dim),
        )
    return values


def product(left_side, right_side):
    return jnp.einsum("bij,bjk->bik", left_side, right_side, precision=lax.Precision.HIGHEST)


def on_device(tokens, grads_out, statistics):
    device = lax.axis_index("tok")
    blocks = statistics.shape[0]
    order_size = statistics.shape[2]
    piece_width = statistics.shape[3]
    pieces = order_size // piece_width
    levels = pieces.bit_length() - 1
    rows_dev = tokens.shape[1] // lax.axis_size("tok")
    side_bit = device // pieces % 2
    column = device % pieces
    slab_index = device % (2 * pieces)

    def columns_of(values):
        return lax.dynamic_slice_in_dim(values, column * piece_width, piece_width, 2)

    core = device % 2
    own_chunks = summed_gradient(tokens, grads_out, device)
    mate_chunks = [swapped(chunk, "tok", 0) for chunk in own_chunks]
    own_half = jnp.concatenate(own_chunks, 0)
    mate_half = jnp.concatenate(mate_chunks, 0)
    gradient = jnp.where(
        core == 0,
        jnp.concatenate([own_half, mate_half], 1),
        jnp.concatenate([mate_half, own_half], 1),
    )
    grad_cube = gradient.reshape(order_size, blocks, order_size)
    forward = jnp.transpose(grad_cube, (1, 0, 2))
    backward = jnp.transpose(grad_cube, (1, 2, 0))
    oriented = jnp.where(side_bit == 0, forward, backward)
    own_rows = lax.dynamic_slice_in_dim(oriented, column * piece_width, piece_width, 1)
    gram_piece = jnp.einsum("brc,bqc->brq", oriented, own_rows, preferred_element_type=jnp.float32)
    fresh_stat = statistics[:, 0] + gram_piece
    identity = jnp.eye(order_size, dtype=jnp.float32)

    def widen(values):
        return doubling(
            values, levels, device, 2, lambda portion, level_bit: swapped(portion, "tok", level_bit)
        )

    assembled = widen(fresh_stat)
    scaling = (2.5 / jnp.sqrt(jnp.sum(assembled * assembled, axis=(1, 2)) + 1e-06))[:, None, None]
    matrix = scaling * assembled
    factor = (5.0 * identity - matrix) * 0.25
    iterate = jnp.sqrt(jnp.sqrt(scaling)) * columns_of(factor)
    for repeat in range(1, ITERS):
        square = widen(product(factor, columns_of(factor)))
        fourth = widen(product(square, columns_of(square)))
        matrix = widen(product(fourth, columns_of(matrix)))
        factor = (5.0 * identity - matrix) * 0.25
        iterate = product(factor, iterate)
    own_root = doubling(
        iterate.astype(jnp.bfloat16),
        levels,
        device,
        2,
        lambda portion, level_bit: swapped(portion, "tok", level_bit),
    )
    other_root = swapped(own_root, "tok", levels)
    left_root = jnp.where(side_bit == 0, own_root, other_root)
    right_root = jnp.where(side_bit == 0, other_root, own_root)
    left_rows = lax.dynamic_slice_in_dim(left_root, slab_index * rows_dev, rows_dev, 1)
    mixed_rows = jnp.einsum(
        "bsr,rbc->bsc", left_rows, grad_cube, preferred_element_type=jnp.float32
    ).astype(jnp.bfloat16)
    update = jnp.einsum(
        "bsc,bcd->sbd", mixed_rows, right_root, preferred_element_type=jnp.float32
    ) * math.sqrt(order_size)
    return (update.reshape(rows_dev, blocks * order_size).astype(jnp.bfloat16), fresh_stat[:, None])


def solution(mesh):
    placed = (P("tok", None), P("tok", "col"), P("col", "tok", None, None))
    return jax.shard_map(
        on_device,
        mesh=mesh,
        in_specs=placed,
        out_specs=(P("tok", "col"), P("col", "tok", None, None)),
        check_vma=False,
    )
```

```python
import functools
import math

import jax
import jax.numpy as jnp
from jax import lax
from jax.experimental import pallas as pl
from jax.experimental.pallas import tpu as pltpu
from jax.sharding import PartitionSpec as P

CHUNKS = (384, 352, 288)
EFFORT = 4


def swapped(block, axis, bit):
    count = lax.axis_size(axis)
    route = []
    for low in range(count):
        high = low | 1 << bit
        if high != low and high < count:
            route += [(low, high), (high, low)]
    return lax.ppermute(block, axis, route)


def ring_sent(block, axis, stride):
    count = lax.axis_size(axis)
    route = []
    for source in range(count):
        step = stride if source % 2 == 0 else -stride
        route.append((source, (source + step) % count))
    return lax.ppermute(block, axis, route)


def regrouped(block, moves):
    route = []
    for base in range(0, lax.axis_size("tok"), 4):
        route += [(base + source, base + target) for source, target in moves]
    return lax.ppermute(block, "tok", route)


def after(value, *events):
    return lax.optimization_barrier((value, *events))[0]


def partial_kernel(kinds, place_ref, *refs):
    count = len(kinds)
    for index, kind in enumerate(kinds):
        picked, grads, partial = refs[index], refs[count + index], refs[2 * count + index]
        partial[...] = matmul(picked[...], grads[...], (0, 0)).astype(kind)


def partial_products(place, tokens, grads_out, blocks, effort):
    order = grads_out.shape[1]
    half = order // 2
    depth = tokens.shape[0]
    tile = 256
    steps = order // tile
    kinds = [jnp.float32 if owner == 0 else jnp.bfloat16 for _, owner in blocks]
    picked = [
        pl.BlockSpec((depth, tile), lambda step, place, where=where: (0, place[where] * steps + step))
        for where, _ in blocks
    ]
    columns = [
        pl.BlockSpec((depth, half), lambda step, place, owner=owner: (0, place[owner])) for _, owner in blocks
    ]
    return pl.pallas_call(
        functools.partial(partial_kernel, kinds),
        out_shape=[jax.ShapeDtypeStruct((order, half), kind) for kind in kinds],
        grid_spec=pltpu.PrefetchScalarGridSpec(
            num_scalar_prefetch=1,
            grid=(steps,),
            in_specs=picked + columns,
            out_specs=[pl.BlockSpec((tile, half), lambda step, place: (step, 0)) for _ in blocks],
        ),
        compiler_params=pltpu.CompilerParams(vmem_limit_bytes=12 << 20),
        cost_estimate=pl.CostEstimate(
            flops=effort * 2 * len(blocks) * order * half * depth,
            bytes_accessed=effort * 6 * len(blocks) * order * half,
            transcendentals=0,
        ),
        name="partial",
    )(place, *[tokens] * len(blocks), *[grads_out] * len(blocks))


def places(device):
    ring = lax.axis_size("tok") // 4
    core = device % 2
    at = device // 4
    turn = 1 - 2 * core
    return jnp.stack(
        [core, 1 - core, (at + turn) % ring, (at - turn) % ring, (at + 2) % ring, at, device // 2 % 2]
    ).astype(jnp.int32)


def block_of_gradient(place, tokens, grads_out, piece, device):
    stride = 4
    starts = [sum(CHUNKS[:index]) for index in range(len(CHUNKS))]
    ahead, behind, across, home = 2, 3, 4, 5
    own, mate = 0, 1
    (given,) = partial_products(place, tokens, grads_out, [(ahead, mate)], 1)
    received = swapped(given, "tok", 0)
    piece = after(piece, given).astype(jnp.bfloat16)
    first = regrouped(piece, [(0, 2), (3, 1), (1, 0), (2, 3)])
    second = regrouped(after(piece, first), [(1, 2), (2, 1)])
    (local,) = partial_products(after(place, given), tokens, grads_out, [(behind, own)], 1)
    totals = [None] * len(CHUNKS)

    def joined(*terms):
        total = terms[0].astype(jnp.float32)
        for term in terms[1:]:
            total = total + term.astype(jnp.float32)
        return total.astype(jnp.bfloat16)

    for k, (start, size) in enumerate(zip(starts, CHUNKS)):
        totals[k] = joined(local[start : start + size], received[start : start + size])
    events = totals
    for hop, (own_block, mate_block) in enumerate(((across, across), (ahead, behind), (home, home))):
        given, local = partial_products(
            after(place, *events), tokens, grads_out, [(mate_block, mate), (own_block, own)], EFFORT
        )
        events = [given, first] if hop == 1 else [given]
        received = swapped(given, "tok", 0)
        for k, (start, size) in enumerate(zip(starts, CHUNKS)):
            arrived = ring_sent(totals[k], "tok", stride)
            if hop == 1 and k == len(CHUNKS) - 1:
                arrived = after(arrived, second)
            totals[k] = joined(local[start : start + size], received[start : start + size], arrived)
    own_chunks = [joined(total, swapped(total, "tok", 1)) for total in totals]
    mate_chunks = [swapped(chunk, "tok", 0) for chunk in own_chunks]
    spot = device % 4
    second = jnp.where((spot == 0) | (spot == 3), piece, second)
    low = jnp.where(spot < 2, second, first)
    high = jnp.where(spot < 2, first, second)
    return own_chunks, mate_chunks, low, high


def iterate_terms():
    terms = [25.0 / 16.0, -5.0 / 16.0, 0.0, 0.0, 0.0, 0.0, 0.0]
    for power in range(6):
        terms[power + 1] -= 0.25 * math.comb(5, power) * 1.25 ** (5 - power) * (-0.25) ** power
    return terms


def matmul(left_side, right_side, contract):
    return lax.dot_general(
        left_side, right_side, ((contract[:1], contract[1:]), ((), ())),
        preferred_element_type=jnp.float32,
    )


TILE = 256


def root_kernel(place_ref, *refs):
    count = len(CHUNKS)
    chunks = refs[: 2 * count]
    low_ref, high_ref, root_ref, own_ref, mate_ref = refs[2 * count : 2 * count + 5]
    stat, work, extra, mat_b, pow_b, cube_b, mix_b = refs[2 * count + 5 :]
    order, half = own_ref.shape
    core = place_ref[0]
    for index, chunk in enumerate(chunks):
        start = sum(CHUNKS[: index % count])
        whole = own_ref if index < count else mate_ref
        whole[pl.ds(start, chunk.shape[0]), :] = chunk[...]
    terms = iterate_terms()
    tiles = [pl.ds(start, TILE) for start in range(0, order, TILE)]

    @pl.when(core == 0)
    def _():
        for tile in tiles:
            gram = matmul(own_ref[tile, :], own_ref[...], (1, 1))
            gram += matmul(mate_ref[tile, :], mate_ref[...], (1, 1))
            stat[tile, :half] = gram[:, :half] + low_ref[tile, :].astype(jnp.float32)
            stat[tile, half:] = gram[:, half:] + high_ref[tile, :].astype(jnp.float32)

    @pl.when(core == 1)
    def _():
        for tile in tiles:
            rows_of = mate_ref if tile.start < half else own_ref
            picked = rows_of[:, pl.ds(tile.start % half, TILE)]
            stat[tile, :half] = matmul(picked, mate_ref[...], (0, 0)) + low_ref[tile, :].astype(jnp.float32)
            stat[tile, half:] = matmul(picked, own_ref[...], (0, 0)) + high_ref[tile, :].astype(jnp.float32)

    total = jnp.zeros((1, order), jnp.float32)
    for tile in tiles:
        values = stat[tile, :]
        total += jnp.sum(values * values, axis=0, keepdims=True)
    total = jnp.sum(total, axis=1, keepdims=True)
    zeta = 2.5 * lax.rsqrt(total + 1e-06)
    for tile in tiles:
        matrix = zeta * stat[tile, :]
        stat[tile, :] = matrix
        mat_b[tile, :] = matrix.astype(jnp.bfloat16)
    for tile in tiles:
        second = matmul(mat_b[tile, :], mat_b[...], (1, 0))
        work[tile, :] = second
        pow_b[tile, :] = second.astype(jnp.bfloat16)
    for tile in tiles:
        third = matmul(mat_b[tile, :], pow_b[...], (1, 0))
        cube_b[tile, :] = third.astype(jnp.bfloat16)
        second = work[tile, :]
        matrix = stat[tile, :]
        mix_b[tile, :] = (terms[6] * third + terms[5] * second + terms[4] * matrix).astype(jnp.bfloat16)
        work[tile, :] = terms[3] * third + terms[2] * second + terms[1] * matrix
    ident = terms[0]
    for tile in tiles:
        rest = work[tile, :] + matmul(mix_b[tile, :], cube_b[...], (1, 0))
        work[tile, :] = rest
        pow_b[tile, :] = rest.astype(jnp.bfloat16)
    for tile in tiles:
        square = matmul(pow_b[tile, :], pow_b[...], (1, 0)) + (2.0 * ident) * work[tile, :]
        mix_b[tile, :] = square.astype(jnp.bfloat16)
    for tile in tiles:
        value = matmul(mat_b[tile, :], mix_b[...], (1, 0)) + (ident * ident) * stat[tile, :]
        extra[tile, :] = value
        cube_b[tile, :] = value.astype(jnp.bfloat16)
    for tile in tiles:
        later = matmul(cube_b[tile, :], mix_b[...], (1, 0)) + (ident * ident) * extra[tile, :]
        mat_b[tile, :] = later.astype(jnp.bfloat16)
        work[tile, :] = 1.25 * work[tile, :] - (0.25 * ident) * later
    scale = jnp.sqrt(jnp.sqrt(zeta))
    for tile in tiles:
        row = lax.broadcasted_iota(jnp.int32, (TILE, order), 0) + tile.start
        column = lax.broadcasted_iota(jnp.int32, (TILE, order), 1)
        rest = work[tile, :] - 0.25 * matmul(pow_b[tile, :], mat_b[...], (1, 0))
        rest = rest + jnp.where(row == column, 1.25 * ident, 0.0)
        root_ref[tile, :] = (scale * rest).astype(jnp.bfloat16)


def stat_kernel(place_ref, own_ref, mate_ref, old_ref, fresh_ref):
    order, half = own_ref.shape
    core = place_ref[0]
    left_chip = place_ref[6]

    @pl.when(left_chip == 0)
    def _():
        picked = pl.ds(pl.multiple_of(core * half, half), half)
        own_rows = own_ref[picked, :]
        mate_rows = mate_ref[picked, :]
        for start in range(0, order, TILE):
            tile = pl.ds(start, TILE)
            gram = matmul(own_ref[tile, :], own_rows, (1, 1)) + matmul(mate_ref[tile, :], mate_rows, (1, 1))
            fresh_ref[tile, :] = old_ref[tile, :] + gram

    @pl.when(left_chip == 1)
    def _():
        own_at = pl.multiple_of(core * half, half)
        mate_at = pl.multiple_of((1 - core) * half, half)
        for start in range(0, half, TILE):
            for rows_of, at in ((own_ref, own_at), (mate_ref, mate_at)):
                tile = pl.ds(at + start, TILE)
                gram = matmul(rows_of[:, pl.ds(start, TILE)], own_ref[...], (0, 0))
                fresh_ref[tile, :] = old_ref[tile, :] + gram


def update_kernel(place_ref, own_ref, mate_ref, own_root_ref, mate_root_ref, update_ref):
    order, half = own_ref.shape
    rows = update_ref.shape[0]
    core = place_ref[0]
    slab = pl.ds(pl.multiple_of((2 * place_ref[6] + core) * rows, rows), rows)

    def finish(first, second, left, right):
        left_rows = left[slab, :]
        mixed_first = matmul(left_rows, first[...], (1, 0)).astype(jnp.bfloat16)
        mixed_second = matmul(left_rows, second[...], (1, 0)).astype(jnp.bfloat16)
        update = matmul(mixed_first, right[:half, :], (1, 0)) + matmul(mixed_second, right[half:, :], (1, 0))
        update_ref[...] = (update * math.sqrt(order)).astype(jnp.bfloat16)

    @pl.when(core == 0)
    def _():
        finish(own_ref, mate_ref, own_root_ref, mate_root_ref)

    @pl.when(core == 1)
    def _():
        finish(mate_ref, own_ref, mate_root_ref, own_root_ref)


VMEM = pl.BlockSpec(memory_space=pltpu.VMEM)
SMEM = pl.BlockSpec(memory_space=pltpu.SMEM)


def on_device(tokens, grads_out, statistics):
    device = lax.axis_index("tok")
    order = statistics.shape[2]
    half = statistics.shape[3]
    rows_dev = tokens.shape[1] // lax.axis_size("tok")
    piece = statistics[0, 0]
    place = places(device)
    tokens = pltpu.with_memory_space_constraint(tokens, pltpu.HBM)
    grads_out = pltpu.with_memory_space_constraint(grads_out, pltpu.HBM)
    own_chunks, mate_chunks, low, high = block_of_gradient(place, tokens, grads_out, piece, device)
    wide = (order, order)
    halves = jax.ShapeDtypeStruct((order, half), jnp.bfloat16)
    own_root, own_half, mate_half = pl.pallas_call(
        root_kernel,
        out_shape=(jax.ShapeDtypeStruct(wide, jnp.bfloat16), halves, halves),
        in_specs=[SMEM] + [VMEM] * (2 * len(CHUNKS) + 2),
        out_specs=(VMEM, VMEM, VMEM),
        scratch_shapes=[pltpu.VMEM(wide, jnp.float32)] * 3 + [pltpu.VMEM(wide, jnp.bfloat16)] * 4,
        compiler_params=pltpu.CompilerParams(vmem_limit_bytes=44 << 20),
        cost_estimate=pl.CostEstimate(flops=16 * order**3, bytes_accessed=8 * order**2, transcendentals=0),
        name="root",
    )(place, *own_chunks, *mate_chunks, low, high)
    mate_root = swapped(own_root, "tok", 0)
    fresh_stat = pl.pallas_call(
        stat_kernel,
        out_shape=jax.ShapeDtypeStruct((order, half), jnp.float32),
        in_specs=[SMEM, VMEM, VMEM, VMEM],
        out_specs=VMEM,
        compiler_params=pltpu.CompilerParams(vmem_limit_bytes=20 << 20),
        cost_estimate=pl.CostEstimate(flops=order**3, bytes_accessed=6 * order**2, transcendentals=0),
        name="statistics",
    )(place, own_half, mate_half, piece)
    update = pl.pallas_call(
        update_kernel,
        out_shape=jax.ShapeDtypeStruct((rows_dev, order), jnp.bfloat16),
        in_specs=[SMEM, VMEM, VMEM, VMEM, VMEM],
        out_specs=VMEM,
        compiler_params=pltpu.CompilerParams(vmem_limit_bytes=20 << 20),
        cost_estimate=pl.CostEstimate(flops=order**3, bytes_accessed=8 * order**2, transcendentals=0),
        name="update",
    )(place, own_half, mate_half, own_root, mate_root)
    return update, fresh_stat[None, None]


def solution(mesh):
    placed = (P("tok", None), P("tok", "col"), P("col", "tok", None, None))
    return jax.shard_map(
        on_device,
        mesh=mesh,
        in_specs=placed,
        out_specs=(P("tok", "col"), P("col", "tok", None, None)),
        check_vma=False,
    )
```

```python
import functools
import math

import jax
import jax.numpy as jnp
from jax import lax
from jax.experimental import pallas as pl
from jax.experimental.pallas import tpu as pltpu
from jax.sharding import PartitionSpec as P

CHUNKS = (656, 368)
EFFORT = 8
TILE = 256
LOAD = 512
VMEM = pl.BlockSpec(memory_space=pltpu.VMEM)
SMEM = pl.BlockSpec(memory_space=pltpu.SMEM)


def swapped(block, axis, bit):
    count = lax.axis_size(axis)
    route = []
    for low in range(count):
        high = low | 1 << bit
        if high != low and high < count:
            route += [(low, high), (high, low)]
    return lax.ppermute(block, axis, route)


def ring_sent(block, axis, stride):
    count = lax.axis_size(axis)
    route = []
    for source in range(count):
        step = stride if source % 2 == 0 else -stride
        route.append((source, (source + step) % count))
    return lax.ppermute(block, axis, route)


def regrouped(block, moves):
    route = []
    for base in range(0, lax.axis_size("tok"), 4):
        route += [(base + source, base + target) for source, target in moves]
    return lax.ppermute(block, "tok", route)


def after(value, *events):
    return lax.optimization_barrier((value, *events))[0]


def partial_kernel(products, loads, staged, place_ref, tokens_ref, grads_ref, *refs):
    order = grads_ref.shape[1]
    half = order // 2
    refs = list(refs)
    blocks = {source: refs.pop(0) for source in sorted({s for s, _ in products if s >= 0})}
    partials = [refs.pop(0) for _ in products]
    loaded = {}
    for handed_on in (True, False):
        for index, (_, kept) in enumerate(loads):
            if kept == handed_on:
                loaded[index] = refs.pop(0)
    semaphores = refs.pop(0)
    copies = {}
    grads_half = None
    if staged:
        grads_half, semaphore = refs
        column = pl.multiple_of(place_ref[products[0][1]] * half, half)
        grads_copy = pltpu.make_async_copy(grads_ref.at[:, pl.ds(column, half)], grads_half, semaphore)
        grads_copy.start()
    for index, (where, _) in enumerate(loads):
        column = place_ref[where] * order
        for piece, start in enumerate(range(0, order, LOAD)):
            copy = pltpu.make_async_copy(
                tokens_ref.at[:, pl.ds(pl.multiple_of(column + start, LOAD), LOAD)],
                loaded[index].at[:, pl.ds(start, LOAD)],
                semaphores.at[index, piece],
            )
            copy.start()
            copies[index, piece] = copy
    if staged:
        grads_copy.wait()
    for start in range(0, order, TILE):
        for (source, owner), partial in zip(products, partials):
            if source < 0:
                block = loaded[-1 - source]
                arriving = copies.pop((-1 - source, start // LOAD), None)
                if arriving is not None:
                    arriving.wait()
            else:
                block = blocks[source]
            if staged:
                grads = grads_half[...]
            else:
                grads = grads_ref[:, pl.ds(pl.multiple_of(place_ref[owner] * half, half), half)]
            product = matmul(block[:, pl.ds(start, TILE)], grads, (0, 0))
            partial[pl.ds(start, TILE), :] = product.astype(partial.dtype)
    for copy in copies.values():
        copy.wait()


def partial_products(place, tokens, grads_out, products, blocks, loads, effort, staged=False):
    depth, order = grads_out.shape
    half = order // 2
    kinds = [jnp.float32 if owner == 0 else jnp.bfloat16 for _, owner in products]
    wide = jax.ShapeDtypeStruct((depth, order), jnp.bfloat16)
    kept = sum(keep for _, keep in loads)
    scratch = [pltpu.VMEM((depth, order), jnp.bfloat16)] * (len(loads) - kept)
    scratch.append(pltpu.SemaphoreType.DMA((max(len(loads), 1), order // LOAD)))
    if staged:
        scratch += [pltpu.VMEM((depth, half), jnp.bfloat16), pltpu.SemaphoreType.DMA]
    memory = pl.BlockSpec(memory_space=pltpu.HBM)
    return pl.pallas_call(
        functools.partial(partial_kernel, products, loads, staged),
        out_shape=[jax.ShapeDtypeStruct((order, half), kind) for kind in kinds] + [wide] * kept,
        in_specs=[SMEM, memory, memory if staged else VMEM] + [VMEM] * len(blocks),
        out_specs=[VMEM] * (len(products) + kept),
        scratch_shapes=scratch,
        compiler_params=pltpu.CompilerParams(vmem_limit_bytes=6 << 20),
        cost_estimate=pl.CostEstimate(
            flops=effort * 2 * len(products) * order * half * depth,
            bytes_accessed=effort * 6 * len(products) * order * half,
            transcendentals=0,
        ),
        name="partial",
    )(place, tokens, grads_out, *blocks)


def pair_kernel(count, where, place_ref, tokens_ref, grads_ref, *refs):
    order = grads_ref.shape[1]
    half = order // 2
    blocks, partials, refs = refs[:count], refs[count : 3 * count], refs[3 * count :]
    copy = None
    if where is not None:
        column = pl.ds(pl.multiple_of(place_ref[where] * order, order), order)
        copy = pltpu.make_async_copy(tokens_ref.at[:, column], refs[0], refs[1])
        copy.start()

    def products(core):
        for index in range(count):
            own, mate = partials[2 * index : 2 * index + 2]
            for start in range(0, order, TILE):
                full = matmul(blocks[index][:, pl.ds(start, TILE)], grads_ref[...], (0, 0))
                at = pl.ds(start, TILE)
                own[at, :] = full[:, core * half : (core + 1) * half]
                mate[at, :] = full[:, (1 - core) * half : (2 - core) * half].astype(jnp.bfloat16)

    for core in range(2):
        pl.when(place_ref[0] == core)(functools.partial(products, core))
    if copy is not None:
        copy.wait()


def pair_products(place, tokens, grads_out, blocks, where, effort):
    depth, order = grads_out.shape
    half = order // 2
    count = len(blocks)
    loaded = [] if where is None else [jax.ShapeDtypeStruct((depth, order), jnp.bfloat16)]
    return pl.pallas_call(
        functools.partial(pair_kernel, count, where),
        out_shape=[jax.ShapeDtypeStruct((order, half), kind) for kind in (jnp.float32, jnp.bfloat16)] * count + loaded,
        in_specs=[SMEM, pl.BlockSpec(memory_space=pltpu.HBM), VMEM] + [VMEM] * count,
        out_specs=[VMEM] * (2 * count + len(loaded)),
        scratch_shapes=[pltpu.SemaphoreType.DMA] * len(loaded),
        compiler_params=pltpu.CompilerParams(vmem_limit_bytes=8 << 20),
        cost_estimate=pl.CostEstimate(
            flops=int(effort * 4 * count * order * half * depth),
            bytes_accessed=int(effort * 12 * count * order * half),
            transcendentals=0,
        ),
        name="pair",
    )(place, tokens, grads_out, *blocks)


def places(device):
    ring = lax.axis_size("tok") // 4
    core = device % 2
    at = device // 4
    turn = 1 - 2 * core
    return jnp.stack(
        [core, 1 - core, (at + turn) % ring, (at - turn) % ring, (at + 2) % ring, at, device // 2 % 2]
    ).astype(jnp.int32)


def block_of_gradient(place, tokens, grads_out, piece, device):
    stride = 4
    starts = [sum(CHUNKS[:index]) for index in range(len(CHUNKS))]
    ahead, behind, across, home = 2, 3, 4, 5
    own, mate = 0, 1
    grads_apart = pltpu.with_memory_space_constraint(grads_out, pltpu.HBM)

    def joined(*terms):
        total = terms[0].astype(jnp.float32)
        for term in terms[1:]:
            total = total + term.astype(jnp.float32)
        return total.astype(jnp.bfloat16)

    def partials(events, *plan):
        return partial_products(after(place, *events), tokens, grads_out, *plan)

    def chunk(values, k):
        return values[starts[k] : starts[k] + CHUNKS[k]]

    def both(local, received, k):
        return chunk(local, k).astype(jnp.float32) + chunk(received, k).astype(jnp.float32)

    given, across_block = partial_products(
        place, tokens, grads_apart, [(-1, mate)], [], [(across, True)], 1, True
    )
    received = swapped(given, "tok", 0)
    local, behind_block, ahead_block = partials(
        [given], [(0, own)], [across_block], [(behind, True), (ahead, True)], 1
    )
    far = joined(local, received)
    piece = after(piece, far).astype(jnp.bfloat16)
    first = regrouped(piece, [(0, 2), (3, 1), (1, 0), (2, 3)])
    second = regrouped(after(piece, first), [(1, 2), (2, 1)])
    local_near, given_on, local_on, given_near, home_block = pair_products(
        after(place, far), tokens, grads_out, [behind_block, ahead_block], home, EFFORT
    )
    far = ring_sent(far, "tok", stride)
    received_on = []
    received_near = []
    for k in range(len(CHUNKS)):
        received_on.append(swapped(chunk(given_on, k), "tok", 0))
        received_near.append(swapped(chunk(given_near, k), "tok", 0))
    local, given = pair_products(after(place, given_near), tokens, grads_out, [home_block], None, 1)
    received = swapped(given, "tok", 0)
    own_chunks = []
    for k in range(len(CHUNKS)):
        near = joined(chunk(local_near, k), received_near[k])
        onward = joined(chunk(local_on, k), received_on[k], chunk(far, k))
        if k > 0:
            near, onward = after(near, received), after(onward, received)
        near = ring_sent(near, "tok", -stride)
        onward = ring_sent(onward, "tok", stride)
        if k == 0:
            near = after(near, first)
        if k == 1:
            near = after(near, second)
        total = joined(both(local, received, k), near, onward)
        own_chunks.append(joined(total, swapped(total, "tok", 1)))
    mate_chunks = [swapped(chunk, "tok", 0) for chunk in own_chunks]
    return own_chunks, mate_chunks, (first, second, piece)


def iterate_terms():
    terms = [25.0 / 16.0, -5.0 / 16.0, 0.0, 0.0, 0.0, 0.0, 0.0]
    for power in range(6):
        terms[power + 1] -= 0.25 * math.comb(5, power) * 1.25 ** (5 - power) * (-0.25) ** power
    return terms


def matmul(left_side, right_side, contract):
    return lax.dot_general(
        left_side, right_side, ((contract[:1], contract[1:]), ((), ())),
        preferred_element_type=jnp.float32,
    )


def root_kernel(place_ref, *refs):
    count = len(CHUNKS)
    chunks = refs[: 2 * count]
    first_ref, second_ref, piece_ref, root_ref, own_ref, mate_ref = refs[2 * count : 2 * count + 6]
    stat, work, extra, mat_b, pow_b, cube_b, mix_b = refs[2 * count + 6 :]
    order, half = own_ref.shape
    for index, chunk in enumerate(chunks):
        start = sum(CHUNKS[: index % count])
        whole = own_ref if index < count else mate_ref
        whole[pl.ds(start, chunk.shape[0]), :] = chunk[...]
    terms = iterate_terms()
    tiles = [pl.ds(start, TILE) for start in range(0, order, TILE)]

    def statistic(core, chip):
        kept = piece_ref if core == chip else second_ref
        low_ref, high_ref = (first_ref, kept) if chip else (kept, first_ref)
        for tile in tiles:
            if core == 0:
                gram = matmul(own_ref[tile, :], own_ref[...], (1, 1))
                gram += matmul(mate_ref[tile, :], mate_ref[...], (1, 1))
                low_gram, high_gram = gram[:, :half], gram[:, half:]
            else:
                rows_of = mate_ref if tile.start < half else own_ref
                picked = rows_of[:, pl.ds(tile.start % half, TILE)]
                low_gram = matmul(picked, mate_ref[...], (0, 0))
                high_gram = matmul(picked, own_ref[...], (0, 0))
            stat[tile, :half] = low_gram + low_ref[tile, :].astype(jnp.float32)
            stat[tile, half:] = high_gram + high_ref[tile, :].astype(jnp.float32)

    for core in range(2):
        for chip in range(2):
            here = (place_ref[0] == core) & (place_ref[6] == chip)
            pl.when(here)(functools.partial(statistic, core, chip))

    total = jnp.zeros((1, order), jnp.float32)
    for tile in tiles:
        values = stat[tile, :]
        total += jnp.sum(values * values, axis=0, keepdims=True)
    total = jnp.sum(total, axis=1, keepdims=True)
    zeta = 2.5 * lax.rsqrt(total + 1e-06)
    for tile in tiles:
        matrix = zeta * stat[tile, :]
        stat[tile, :] = matrix
        mat_b[tile, :] = matrix.astype(jnp.bfloat16)
    for tile in tiles:
        second = matmul(mat_b[tile, :], mat_b[...], (1, 0))
        work[tile, :] = second
        pow_b[tile, :] = second.astype(jnp.bfloat16)
    for tile in tiles:
        third = matmul(mat_b[tile, :], pow_b[...], (1, 0))
        cube_b[tile, :] = third.astype(jnp.bfloat16)
        second = work[tile, :]
        matrix = stat[tile, :]
        mix_b[tile, :] = (terms[6] * third + terms[5] * second + terms[4] * matrix).astype(jnp.bfloat16)
        work[tile, :] = terms[3] * third + terms[2] * second + terms[1] * matrix
    ident = terms[0]
    for tile in tiles:
        rest = work[tile, :] + matmul(mix_b[tile, :], cube_b[...], (1, 0))
        work[tile, :] = rest
        pow_b[tile, :] = rest.astype(jnp.bfloat16)
    for tile in tiles:
        square = matmul(pow_b[tile, :], pow_b[...], (1, 0)) + (2.0 * ident) * work[tile, :]
        mix_b[tile, :] = square.astype(jnp.bfloat16)
    for tile in tiles:
        value = matmul(mat_b[tile, :], mix_b[...], (1, 0)) + (ident * ident) * stat[tile, :]
        extra[tile, :] = value
        cube_b[tile, :] = value.astype(jnp.bfloat16)
    for tile in tiles:
        later = matmul(cube_b[tile, :], mix_b[...], (1, 0)) + (ident * ident) * extra[tile, :]
        mat_b[tile, :] = later.astype(jnp.bfloat16)
        work[tile, :] = 1.25 * work[tile, :] - (0.25 * ident) * later
    scale = jnp.sqrt(jnp.sqrt(zeta))
    for tile in tiles:
        row = lax.broadcasted_iota(jnp.int32, (TILE, order), 0) + tile.start
        column = lax.broadcasted_iota(jnp.int32, (TILE, order), 1)
        rest = work[tile, :] - 0.25 * matmul(pow_b[tile, :], mat_b[...], (1, 0))
        rest = rest + jnp.where(row == column, 1.25 * ident, 0.0)
        root_ref[tile, :] = (scale * rest).astype(jnp.bfloat16)


def stat_kernel(place_ref, own_ref, mate_ref, old_ref, fresh_ref):
    order, half = own_ref.shape
    core = place_ref[0]
    left_chip = place_ref[6]

    @pl.when(left_chip == 0)
    def _():
        picked = pl.ds(pl.multiple_of(core * half, half), half)
        own_rows = own_ref[picked, :]
        mate_rows = mate_ref[picked, :]
        for start in range(0, order, TILE):
            tile = pl.ds(start, TILE)
            gram = matmul(own_ref[tile, :], own_rows, (1, 1)) + matmul(mate_ref[tile, :], mate_rows, (1, 1))
            fresh_ref[tile, :] = old_ref[tile, :] + gram

    @pl.when(left_chip == 1)
    def _():
        own_at = pl.multiple_of(core * half, half)
        mate_at = pl.multiple_of((1 - core) * half, half)
        for start in range(0, half, TILE):
            for rows_of, at in ((own_ref, own_at), (mate_ref, mate_at)):
                tile = pl.ds(at + start, TILE)
                gram = matmul(rows_of[:, pl.ds(start, TILE)], own_ref[...], (0, 0))
                fresh_ref[tile, :] = old_ref[tile, :] + gram


def update_kernel(place_ref, own_ref, mate_ref, own_root_ref, mate_root_ref, update_ref):
    order, half = own_ref.shape
    rows = update_ref.shape[0]
    core = place_ref[0]
    slab = pl.ds(pl.multiple_of((2 * place_ref[6] + core) * rows, rows), rows)

    def finish(first, second, left, right):
        left_rows = left[slab, :]
        mixed_first = matmul(left_rows, first[...], (1, 0)).astype(jnp.bfloat16)
        mixed_second = matmul(left_rows, second[...], (1, 0)).astype(jnp.bfloat16)
        update = matmul(mixed_first, right[:half, :], (1, 0)) + matmul(mixed_second, right[half:, :], (1, 0))
        update_ref[...] = (update * math.sqrt(order)).astype(jnp.bfloat16)

    @pl.when(core == 0)
    def _():
        finish(own_ref, mate_ref, own_root_ref, mate_root_ref)

    @pl.when(core == 1)
    def _():
        finish(mate_ref, own_ref, mate_root_ref, own_root_ref)


def on_device(tokens, grads_out, statistics):
    device = lax.axis_index("tok")
    order = statistics.shape[2]
    half = statistics.shape[3]
    rows_dev = tokens.shape[1] // lax.axis_size("tok")
    piece = statistics[0, 0]
    place = places(device)
    tokens = pltpu.with_memory_space_constraint(tokens, pltpu.HBM)
    own_chunks, mate_chunks, old_pieces = block_of_gradient(place, tokens, grads_out, piece, device)
    wide = (order, order)
    halves = jax.ShapeDtypeStruct((order, half), jnp.bfloat16)
    own_root, own_half, mate_half = pl.pallas_call(
        root_kernel,
        out_shape=(jax.ShapeDtypeStruct(wide, jnp.bfloat16), halves, halves),
        in_specs=[SMEM] + [VMEM] * (2 * len(CHUNKS) + 3),
        out_specs=(VMEM, VMEM, VMEM),
        scratch_shapes=[pltpu.VMEM(wide, jnp.float32)] * 3 + [pltpu.VMEM(wide, jnp.bfloat16)] * 4,
        compiler_params=pltpu.CompilerParams(vmem_limit_bytes=36 << 20),
        cost_estimate=pl.CostEstimate(flops=16 * order**3, bytes_accessed=8 * order**2, transcendentals=0),
        name="root",
    )(place, *own_chunks, *mate_chunks, *old_pieces)
    mate_root = swapped(own_root, "tok", 0)
    fresh_stat = pl.pallas_call(
        stat_kernel,
        out_shape=jax.ShapeDtypeStruct((order, half), jnp.float32),
        in_specs=[SMEM, VMEM, VMEM, VMEM],
        out_specs=VMEM,
        compiler_params=pltpu.CompilerParams(vmem_limit_bytes=8 << 20),
        cost_estimate=pl.CostEstimate(flops=order**3, bytes_accessed=6 * order**2, transcendentals=0),
        name="statistics",
    )(place, own_half, mate_half, piece)
    update = pl.pallas_call(
        update_kernel,
        out_shape=jax.ShapeDtypeStruct((rows_dev, order), jnp.bfloat16),
        in_specs=[SMEM, VMEM, VMEM, VMEM, VMEM],
        out_specs=VMEM,
        compiler_params=pltpu.CompilerParams(vmem_limit_bytes=8 << 20),
        cost_estimate=pl.CostEstimate(flops=order**3, bytes_accessed=8 * order**2, transcendentals=0),
        name="update",
    )(place, own_half, mate_half, own_root, mate_root)
    return update, fresh_stat[None, None]


def solution(mesh):
    placed = (P("tok", None), P("tok", "col"), P("col", "tok", None, None))
    return jax.shard_map(
        on_device,
        mesh=mesh,
        in_specs=placed,
        out_specs=(P("tok", "col"), P("col", "tok", None, None)),
        check_vma=False,
    )
```

```python
import functools
import math

import jax
import jax.numpy as jnp
from jax import lax
from jax.experimental import pallas as pl
from jax.experimental.pallas import tpu as pltpu
from jax.sharding import PartitionSpec as P

CHUNKS = (528, 496)
EFFORT = 8
TILE = 256
LOAD = 512
VMEM = pl.BlockSpec(memory_space=pltpu.VMEM)
SMEM = pl.BlockSpec(memory_space=pltpu.SMEM)


def swapped(block, axis, bit):
    count = lax.axis_size(axis)
    route = []
    for low in range(count):
        high = low | 1 << bit
        if high != low and high < count:
            route += [(low, high), (high, low)]
    return lax.ppermute(block, axis, route)


def ring_sent(block, axis, stride):
    count = lax.axis_size(axis)
    route = []
    for source in range(count):
        step = stride if source % 2 == 0 else -stride
        route.append((source, (source + step) % count))
    return lax.ppermute(block, axis, route)


def regrouped(block, moves):
    route = []
    for base in range(0, lax.axis_size("tok"), 4):
        route += [(base + source, base + target) for source, target in moves]
    return lax.ppermute(block, "tok", route)


def after(value, *events):
    return lax.optimization_barrier((value, *events))[0]


def partial_kernel(products, loads, staged, place_ref, tokens_ref, grads_ref, *refs):
    order = grads_ref.shape[1]
    half = order // 2
    refs = list(refs)
    blocks = {source: refs.pop(0) for source in sorted({s for s, _ in products if s >= 0})}
    partials = [refs.pop(0) for _ in products]
    loaded = {}
    for handed_on in (True, False):
        for index, (_, kept) in enumerate(loads):
            if kept == handed_on:
                loaded[index] = refs.pop(0)
    semaphores = refs.pop(0)
    copies = {}
    grads_half = None
    if staged:
        grads_half, semaphore = refs
        column = pl.multiple_of(place_ref[products[0][1]] * half, half)
        grads_copy = pltpu.make_async_copy(grads_ref.at[:, pl.ds(column, half)], grads_half, semaphore)
        grads_copy.start()
    for index, (where, _) in enumerate(loads):
        column = place_ref[where] * order
        for piece, start in enumerate(range(0, order, LOAD)):
            copy = pltpu.make_async_copy(
                tokens_ref.at[:, pl.ds(pl.multiple_of(column + start, LOAD), LOAD)],
                loaded[index].at[:, pl.ds(start, LOAD)],
                semaphores.at[index, piece],
            )
            copy.start()
            copies[index, piece] = copy
    if staged:
        grads_copy.wait()
    for start in range(0, order, TILE):
        for (source, owner), partial in zip(products, partials):
            if source < 0:
                block = loaded[-1 - source]
                arriving = copies.pop((-1 - source, start // LOAD), None)
                if arriving is not None:
                    arriving.wait()
            else:
                block = blocks[source]
            if staged:
                grads = grads_half[...]
            else:
                grads = grads_ref[:, pl.ds(pl.multiple_of(place_ref[owner] * half, half), half)]
            product = matmul(block[:, pl.ds(start, TILE)], grads, (0, 0))
            partial[pl.ds(start, TILE), :] = product.astype(partial.dtype)
    for copy in copies.values():
        copy.wait()


def partial_products(place, tokens, grads_out, products, blocks, loads, effort, staged=False):
    depth, order = grads_out.shape
    half = order // 2
    kinds = [jnp.float32 if owner == 0 else jnp.bfloat16 for _, owner in products]
    wide = jax.ShapeDtypeStruct((depth, order), jnp.bfloat16)
    kept = sum(keep for _, keep in loads)
    scratch = [pltpu.VMEM((depth, order), jnp.bfloat16)] * (len(loads) - kept)
    scratch.append(pltpu.SemaphoreType.DMA((max(len(loads), 1), order // LOAD)))
    if staged:
        scratch += [pltpu.VMEM((depth, half), jnp.bfloat16), pltpu.SemaphoreType.DMA]
    memory = pl.BlockSpec(memory_space=pltpu.HBM)
    return pl.pallas_call(
        functools.partial(partial_kernel, products, loads, staged),
        out_shape=[jax.ShapeDtypeStruct((order, half), kind) for kind in kinds] + [wide] * kept,
        in_specs=[SMEM, memory, memory if staged else VMEM] + [VMEM] * len(blocks),
        out_specs=[VMEM] * (len(products) + kept),
        scratch_shapes=scratch,
        compiler_params=pltpu.CompilerParams(vmem_limit_bytes=6 << 20),
        cost_estimate=pl.CostEstimate(
            flops=effort * 2 * len(products) * order * half * depth,
            bytes_accessed=effort * 6 * len(products) * order * half,
            transcendentals=0,
        ),
        name="partial",
    )(place, tokens, grads_out, *blocks)


def pair_kernel(count, wheres, place_ref, tokens_ref, grads_ref, *refs):
    order = grads_ref.shape[1]
    half = order // 2
    total = count + len(wheres[:1])
    blocks, partials, refs = list(refs[:count]), refs[count : count + 2 * total], refs[count + 2 * total :]
    copies = []
    for index, where in enumerate(wheres):
        column = pl.ds(pl.multiple_of(place_ref[where] * order, order), order)
        loaded = refs[1 - index]
        copies.append(pltpu.make_async_copy(tokens_ref.at[:, column], loaded, refs[2 + index]))
        copies[-1].start()
    if wheres:
        blocks.append(refs[1])

    def products(core):
        for index, block in enumerate(blocks):
            if index == count:
                copies[0].wait()
            own, mate = partials[2 * index : 2 * index + 2]

            def tile_product(step, _, block=block, own=own, mate=mate):
                at = pl.ds(pl.multiple_of(step * TILE, TILE), TILE)
                full = matmul(block[:, at], grads_ref[...], (0, 0))
                own[at, :] = full[:, core * half : (core + 1) * half]
                mate[at, :] = full[:, (1 - core) * half : (2 - core) * half].astype(jnp.bfloat16)
                return 0

            lax.fori_loop(0, order // TILE, tile_product, 0)

    for core in range(2):
        pl.when(place_ref[0] == core)(functools.partial(products, core))
    for copy in copies[1:]:
        copy.wait()


def pair_products(place, tokens, grads_out, blocks, wheres, effort):
    depth, order = grads_out.shape
    half = order // 2
    total = len(blocks) + len(wheres[:1])
    handed_on = len(wheres[1:])
    return pl.pallas_call(
        functools.partial(pair_kernel, len(blocks), wheres),
        out_shape=[jax.ShapeDtypeStruct((order, half), kind) for kind in (jnp.float32, jnp.bfloat16)] * total
        + [jax.ShapeDtypeStruct((depth, order), jnp.bfloat16)] * handed_on,
        in_specs=[SMEM, pl.BlockSpec(memory_space=pltpu.HBM), VMEM] + [VMEM] * len(blocks),
        out_specs=[VMEM] * (2 * total + handed_on),
        scratch_shapes=[pltpu.VMEM((depth, order), jnp.bfloat16)] * len(wheres[:1])
        + [pltpu.SemaphoreType.DMA] * len(wheres),
        compiler_params=pltpu.CompilerParams(vmem_limit_bytes=8 << 20),
        cost_estimate=pl.CostEstimate(
            flops=effort * 4 * total * order * half * depth,
            bytes_accessed=effort * 12 * total * order * half,
            transcendentals=0,
        ),
        name="pair",
    )(place, tokens, grads_out, *blocks)


def places(device):
    ring = lax.axis_size("tok") // 4
    core = device % 2
    at = device // 4
    turn = 1 - 2 * core
    return jnp.stack(
        [core, 1 - core, (at + turn) % ring, (at - turn) % ring, (at + 2) % ring, at, device // 2 % 2]
    ).astype(jnp.int32)


def block_of_gradient(place, tokens, grads_out, piece, device):
    stride = 4
    starts = [sum(CHUNKS[:index]) for index in range(len(CHUNKS))]
    ahead, behind, across, home = 2, 3, 4, 5
    own, mate = 0, 1
    grads_apart = pltpu.with_memory_space_constraint(grads_out, pltpu.HBM)

    def joined(*terms):
        total = terms[0].astype(jnp.float32)
        for term in terms[1:]:
            total = total + term.astype(jnp.float32)
        return total.astype(jnp.bfloat16)

    def partials(events, *plan):
        return partial_products(after(place, *events), tokens, grads_out, *plan)

    def chunk(values, k):
        return values[starts[k] : starts[k] + CHUNKS[k]]

    def both(local, received, k):
        return chunk(local, k).astype(jnp.float32) + chunk(received, k).astype(jnp.float32)

    given, across_block = partial_products(
        place, tokens, grads_apart, [(-1, mate)], [], [(across, True)], 1, True
    )
    received = swapped(given, "tok", 0)
    local, behind_block = partials([given], [(0, own)], [across_block], [(behind, True)], 1)
    far = joined(local, received)
    piece = after(piece, far).astype(jnp.bfloat16)
    first = regrouped(piece, [(0, 2), (3, 1), (1, 0), (2, 3)])
    second = regrouped(after(piece, first), [(1, 2), (2, 1)])
    local_near, given_on, local_on, given_near, home_block = pair_products(
        after(place, far), tokens, grads_out, [behind_block], (ahead, home), EFFORT
    )
    far = ring_sent(far, "tok", stride)
    received_on = []
    received_near = []
    for k in range(len(CHUNKS)):
        received_on.append(swapped(chunk(given_on, k), "tok", 0))
        received_near.append(swapped(chunk(given_near, k), "tok", 0))
    local, given = pair_products(after(place, given_near), tokens, grads_out, [home_block], (), 1)
    received = swapped(given, "tok", 0)
    own_chunks = []
    for k in range(len(CHUNKS)):
        near = joined(chunk(local_near, k), received_near[k])
        onward = joined(chunk(local_on, k), received_on[k], chunk(far, k))
        if k > 0:
            near, onward = after(near, received), after(onward, received)
        near = ring_sent(near, "tok", -stride)
        onward = ring_sent(onward, "tok", stride)
        near = after(near, second if k else first)
        total = joined(both(local, received, k), near, onward)
        own_chunks.append(joined(total, swapped(total, "tok", 1)))
    mate_chunks = [swapped(chunk, "tok", 0) for chunk in own_chunks]
    return own_chunks, mate_chunks, (first, second, piece)


def iterate_terms():
    terms = [25.0 / 16.0, -5.0 / 16.0, 0.0, 0.0, 0.0, 0.0, 0.0]
    for power in range(6):
        terms[power + 1] -= 0.25 * math.comb(5, power) * 1.25 ** (5 - power) * (-0.25) ** power
    return terms


def matmul(left_side, right_side, contract):
    return lax.dot_general(
        left_side, right_side, ((contract[:1], contract[1:]), ((), ())),
        preferred_element_type=jnp.float32,
    )


def root_kernel(place_ref, *refs):
    count = len(CHUNKS)
    chunks = refs[: 2 * count]
    first_ref, second_ref, piece_ref, root_ref, own_ref, mate_ref = refs[2 * count : 2 * count + 6]
    stat, work, extra, mat_b, pow_b, cube_b, mix_b = refs[2 * count + 6 :]
    order, half = own_ref.shape
    for index, chunk in enumerate(chunks):
        start = sum(CHUNKS[: index % count])
        whole = own_ref if index < count else mate_ref
        whole[pl.ds(start, chunk.shape[0]), :] = chunk[...]
    terms = iterate_terms()
    tiles = [pl.ds(start, TILE) for start in range(0, order, TILE)]

    def old_statistic(core, chip):
        kept = piece_ref if core == chip else second_ref
        low_ref, high_ref = (first_ref, kept) if chip else (kept, first_ref)

        def copied(step, _):
            tile = pl.ds(pl.multiple_of(step * 64, 64), 64)
            stat[tile, :half] = low_ref[tile, :].astype(jnp.float32)
            stat[tile, half:] = high_ref[tile, :].astype(jnp.float32)
            return 0

        lax.fori_loop(0, order // 64, copied, 0)

    for core in range(2):
        for chip in range(2):
            here = (place_ref[0] == core) & (place_ref[6] == chip)
            pl.when(here)(functools.partial(old_statistic, core, chip))

    @pl.when(place_ref[0] == 0)
    def _():
        def left(step, _):
            tile = pl.ds(pl.multiple_of(step * TILE, TILE), TILE)
            gram = matmul(own_ref[tile, :], own_ref[...], (1, 1))
            gram += matmul(mate_ref[tile, :], mate_ref[...], (1, 1))
            stat[tile, :] += gram
            return 0

        lax.fori_loop(0, order // TILE, left, 0)

    @pl.when(place_ref[0] == 1)
    def _():
        for rows_of, first_row in ((mate_ref, 0), (own_ref, half)):

            def right(step, _, rows_of=rows_of, first_row=first_row):
                at = pl.multiple_of(step * TILE, TILE)
                tile = pl.ds(pl.multiple_of(first_row + at, TILE), TILE)
                picked = rows_of[:, pl.ds(at, TILE)]
                stat[tile, :half] += matmul(picked, mate_ref[...], (0, 0))
                stat[tile, half:] += matmul(picked, own_ref[...], (0, 0))
                return 0

            lax.fori_loop(0, half // TILE, right, 0)

    total = jnp.zeros((1, order), jnp.float32)
    for tile in tiles:
        values = stat[tile, :]
        total += jnp.sum(values * values, axis=0, keepdims=True)
    total = jnp.sum(total, axis=1, keepdims=True)
    zeta = 2.5 * lax.rsqrt(total + 1e-06)
    for tile in tiles:
        matrix = zeta * stat[tile, :]
        stat[tile, :] = matrix
        mat_b[tile, :] = matrix.astype(jnp.bfloat16)
    for tile in tiles:
        second = matmul(mat_b[tile, :], mat_b[...], (1, 0))
        work[tile, :] = second
        pow_b[tile, :] = second.astype(jnp.bfloat16)
    for tile in tiles:
        third = matmul(mat_b[tile, :], pow_b[...], (1, 0))
        cube_b[tile, :] = third.astype(jnp.bfloat16)
        second = work[tile, :]
        matrix = stat[tile, :]
        mix_b[tile, :] = (terms[6] * third + terms[5] * second + terms[4] * matrix).astype(jnp.bfloat16)
        work[tile, :] = terms[3] * third + terms[2] * second + terms[1] * matrix
    ident = terms[0]
    for tile in tiles:
        rest = work[tile, :] + matmul(mix_b[tile, :], cube_b[...], (1, 0))
        work[tile, :] = rest
        pow_b[tile, :] = rest.astype(jnp.bfloat16)
    for tile in tiles:
        square = matmul(pow_b[tile, :], pow_b[...], (1, 0)) + (2.0 * ident) * work[tile, :]
        mix_b[tile, :] = square.astype(jnp.bfloat16)
    for tile in tiles:
        value = matmul(mat_b[tile, :], mix_b[...], (1, 0)) + (ident * ident) * stat[tile, :]
        extra[tile, :] = value
        cube_b[tile, :] = value.astype(jnp.bfloat16)
    for tile in tiles:
        later = matmul(cube_b[tile, :], mix_b[...], (1, 0)) + (ident * ident) * extra[tile, :]
        mat_b[tile, :] = later.astype(jnp.bfloat16)
        work[tile, :] = 1.25 * work[tile, :] - (0.25 * ident) * later
    scale = jnp.sqrt(jnp.sqrt(zeta))
    for tile in tiles:
        row = lax.broadcasted_iota(jnp.int32, (TILE, order), 0) + tile.start
        column = lax.broadcasted_iota(jnp.int32, (TILE, order), 1)
        rest = work[tile, :] - 0.25 * matmul(pow_b[tile, :], mat_b[...], (1, 0))
        rest = rest + jnp.where(row == column, 1.25 * ident, 0.0)
        root_ref[tile, :] = (scale * rest).astype(jnp.bfloat16)


def stat_kernel(place_ref, own_ref, mate_ref, old_ref, fresh_ref):
    order, half = own_ref.shape
    core = place_ref[0]
    left_chip = place_ref[6]

    @pl.when(left_chip == 0)
    def _():
        picked = pl.ds(pl.multiple_of(core * half, half), half)

        def left(step, _):
            tile = pl.ds(pl.multiple_of(step * TILE, TILE), TILE)
            gram = matmul(own_ref[tile, :], own_ref[picked, :], (1, 1))
            gram += matmul(mate_ref[tile, :], mate_ref[picked, :], (1, 1))
            fresh_ref[tile, :] = old_ref[tile, :] + gram
            return 0

        lax.fori_loop(0, order // TILE, left, 0)

    @pl.when(left_chip == 1)
    def _():
        for rows_of, first_row in ((own_ref, core * half), (mate_ref, (1 - core) * half)):

            def right(step, _, rows_of=rows_of, first_row=first_row):
                at = pl.multiple_of(step * TILE, TILE)
                tile = pl.ds(pl.multiple_of(first_row + at, TILE), TILE)
                gram = matmul(rows_of[:, pl.ds(at, TILE)], own_ref[...], (0, 0))
                fresh_ref[tile, :] = old_ref[tile, :] + gram
                return 0

            lax.fori_loop(0, half // TILE, right, 0)


def update_kernel(place_ref, own_ref, mate_ref, own_root_ref, mate_root_ref, update_ref):
    order, half = own_ref.shape
    rows = update_ref.shape[0]
    core = place_ref[0]
    slab = pl.ds(pl.multiple_of((2 * place_ref[6] + core) * rows, rows), rows)

    def finish(first, second, left, right):
        left_rows = left[slab, :]
        mixed_first = matmul(left_rows, first[...], (1, 0)).astype(jnp.bfloat16)
        mixed_second = matmul(left_rows, second[...], (1, 0)).astype(jnp.bfloat16)
        update = matmul(mixed_first, right[:half, :], (1, 0)) + matmul(mixed_second, right[half:, :], (1, 0))
        update_ref[...] = (update * math.sqrt(order)).astype(jnp.bfloat16)

    @pl.when(core == 0)
    def _():
        finish(own_ref, mate_ref, own_root_ref, mate_root_ref)

    @pl.when(core == 1)
    def _():
        finish(mate_ref, own_ref, mate_root_ref, own_root_ref)


def on_device(tokens, grads_out, statistics):
    device = lax.axis_index("tok")
    order = statistics.shape[2]
    half = statistics.shape[3]
    rows_dev = tokens.shape[1] // lax.axis_size("tok")
    piece = statistics[0, 0]
    place = places(device)
    tokens = pltpu.with_memory_space_constraint(tokens, pltpu.HBM)
    own_chunks, mate_chunks, old_pieces = block_of_gradient(place, tokens, grads_out, piece, device)
    wide = (order, order)
    halves = jax.ShapeDtypeStruct((order, half), jnp.bfloat16)
    own_root, own_half, mate_half = pl.pallas_call(
        root_kernel,
        out_shape=(jax.ShapeDtypeStruct(wide, jnp.bfloat16), halves, halves),
        in_specs=[SMEM] + [VMEM] * (2 * len(CHUNKS) + 3),
        out_specs=(VMEM, VMEM, VMEM),
        scratch_shapes=[pltpu.VMEM(wide, jnp.float32)] * 3 + [pltpu.VMEM(wide, jnp.bfloat16)] * 4,
        compiler_params=pltpu.CompilerParams(vmem_limit_bytes=36 << 20),
        cost_estimate=pl.CostEstimate(flops=16 * order**3, bytes_accessed=8 * order**2, transcendentals=0),
        name="root",
    )(place, *own_chunks, *mate_chunks, *old_pieces)
    mate_root = swapped(own_root, "tok", 0)
    fresh_stat = pl.pallas_call(
        stat_kernel,
        out_shape=jax.ShapeDtypeStruct((order, half), jnp.float32),
        in_specs=[SMEM, VMEM, VMEM, VMEM],
        out_specs=VMEM,
        compiler_params=pltpu.CompilerParams(vmem_limit_bytes=8 << 20),
        cost_estimate=pl.CostEstimate(flops=order**3, bytes_accessed=6 * order**2, transcendentals=0),
        name="statistics",
    )(place, own_half, mate_half, piece)
    update = pl.pallas_call(
        update_kernel,
        out_shape=jax.ShapeDtypeStruct((rows_dev, order), jnp.bfloat16),
        in_specs=[SMEM, VMEM, VMEM, VMEM, VMEM],
        out_specs=VMEM,
        compiler_params=pltpu.CompilerParams(vmem_limit_bytes=8 << 20),
        cost_estimate=pl.CostEstimate(flops=order**3, bytes_accessed=8 * order**2, transcendentals=0),
        name="update",
    )(place, own_half, mate_half, own_root, mate_root)
    return update, fresh_stat[None, None]


def solution(mesh):
    placed = (P("tok", None), P("tok", "col"), P("col", "tok", None, None))
    return jax.shard_map(
        on_device,
        mesh=mesh,
        in_specs=placed,
        out_specs=(P("tok", "col"), P("col", "tok", None, None)),
        check_vma=False,
    )
```
